32 devices in a mesh: prow: 4 (over z), pcol: 8 (over y, x, core).
Axes of the slice: x: 2, y: 2, z: 4, core: 2. Of those that a mesh axis runs over, the one named last changes fastest.
Arguments:
- anc_inverse: float32 [2048, 2048], P('pcol', 'prow')
- pattern_one: int32 [8, 4], replicated, may hold values from 0 to 7, as said below
- parents: int32 [8], replicated, may hold values from 0 to 7, as said below
- low_one: float32 [8, 1024, 256], P('pcol', 'prow'), may hold values from -2 to 2
- pivot_one: float32 [8, 256, 256], P('pcol'), may hold values from -4 to 4
- low_two: float32 [8, 1024, 256], P('pcol', 'prow'), may hold values from -2 to 2
- second_scaled_factor: float32 [8, 256, 256], P('pcol'), may hold values from -2 to 2
- second_pivot_inverse: float32 [8, 256, 256], P('pcol'), may hold values from -4 to 4
Outputs:
- column_one: float32 [8, 2048, 256], P('prow', 'pcol')
- diag_one: float32 [8, 256, 256], P('pcol')
- column_two: float32 [8, 2048, 256], P('prow', 'pcol')
- second_parent_inverse: float32 [8, 256, 256], P('pcol')
- second_diagonal_inverse: float32 [8, 256, 256], P('pcol')
The draws below stay inside these ranges and needn't reach their ends.
Inputs may be any that keep to these rules, and one draw needn't show every extreme that they name: `pattern_one`: entry r of each row names an ancestor of process row r: it lies in r * 2 to r * 2 + 1; for each r, every ancestor of that range is entry r of exactly 4 rows. `parents`: every first-level supernode is the parent of exactly one second-level supernode.
All inputs are finite; a program needn't handle non-finite values.
Results may differ from the reference program's by a relative error of at most 0.000073.
Values sent between devices are 32-bit elements; how exact they have to be, the bound alone decides.
A program may use at most 128 MiB of HBM per device.

```python
import jax
import jax.numpy as jnp
from jax import lax

B = 256
NA = 8
P_SIZE = 4
CB = 2
K1 = 8
M2 = 8


def draw_anc_inverse(key, part):
    total = NA * B
    noise = jax.random.normal(key, (total, total), jnp.float32)
    symmetric = (noise + noise.T) * (0.35 / jnp.sqrt(2.0 * total))
    return jnp.eye(total, dtype=jnp.float32) + symmetric


def draw_pattern_one(key, part):
    column_keys = jax.random.split(jax.random.fold_in(key, 17), P_SIZE)
    base = (jnp.arange(K1, dtype=jnp.int32) % CB).astype(jnp.int32)
    offsets = jax.vmap(lambda k: jax.random.permutation(k, base))(column_keys).T
    starts = jnp.arange(P_SIZE, dtype=jnp.int32)[None, :] * CB
    return (offsets + starts).astype(jnp.int32)


def draw_parents(key, part):
    base = (jnp.arange(M2, dtype=jnp.int32) % K1).astype(jnp.int32)
    return jax.random.permutation(jax.random.fold_in(key, 29), base).astype(jnp.int32)


def block_levels(rng, shape, cuts, least, high):
    def one(position, shards_of):
        heights = jax.random.uniform(jax.random.fold_in(jax.random.fold_in(rng, 6), position), (shards_of,), jnp.float32, least / len(cuts), high / len(cuts))
        return jnp.repeat(jnp.exp(heights), shape[position] // shards_of).reshape((-1,) + (1,) * (len(shape) - position - 1))

    gain = one(*cuts[0])
    for cut in cuts[1:]:
        gain = gain * one(*cut)
    return gain


def gaussian(key, dims, scale, limit, cuts=(), kind=jnp.bfloat16):
    result = scale * jax.random.normal(key, dims, jnp.float32)
    if cuts:
        result = result * block_levels(key, dims, cuts, -0.22, 0.18)
    return jnp.clip(result, -limit, limit).astype(kind)


def setup_inputs(seed: int = 0) -> dict:
    splits = jax.random.split(jax.random.key(seed), 9)
    anc_inverse = draw_anc_inverse(jax.random.fold_in(splits[8], 71), 0)
    pattern_one = draw_pattern_one(jax.random.fold_in(splits[8], 71), 0)
    parents = draw_parents(jax.random.fold_in(splits[8], 71), 0)
    low_one = gaussian(splits[3], (K1, P_SIZE * B, B), 0.15, 2.0, ((0, 8), (1, 4)), jnp.float32)
    pivot_one = gaussian(splits[4], (K1, B, B), 0.3, 4.0, ((0, 8),), jnp.float32)
    low_two = gaussian(splits[5], (M2, P_SIZE * B, B), 0.15, 2.0, ((0, 8), (1, 4)), jnp.float32)
    second_scaled_factor = gaussian(splits[6], (M2, B, B), 0.15, 2.0, ((0, 8),), jnp.float32)
    second_pivot_inverse = gaussian(splits[7], (M2, B, B), 0.3, 4.0, ((0, 8),), jnp.float32)
    return {"anc_inverse": anc_inverse, "pattern_one": pattern_one, "parents": parents, "low_one": low_one, "pivot_one": pivot_one, "low_two": low_two, "second_scaled_factor": second_scaled_factor, "second_pivot_inverse": second_pivot_inverse}


def reference(anc_inverse, pattern_one, parents, low_one, pivot_one, low_two, second_scaled_factor, second_pivot_inverse):
    highest_accuracy = lax.Precision.HIGHEST
    blocks = anc_inverse.reshape(NA, B, NA, B).transpose(0, 2, 1, 3)
    lower_one = low_one.reshape(K1, P_SIZE, B, B)
    lower_two = low_two.reshape(M2, P_SIZE, B, B)

    def first_column(args):
        slots, factor = args
        chosen = blocks[:, slots]
        return -jnp.einsum('iprs,pst->irt', chosen, factor, precision=highest_accuracy)

    column_full = lax.map(first_column, (pattern_one, lower_one))
    on_slots = jax.vmap(lambda z, s: z[s])(column_full, pattern_one)
    diag_one = pivot_one - jnp.einsum('kpsa,kpsb->kab', lower_one, on_slots, precision=highest_accuracy)

    pattern_two = pattern_one[parents]
    parent_column = column_full[parents]

    def second_column(args):
        slots, factor, upper, parent_block = args
        chosen = blocks[:, slots]
        local_sum = jnp.einsum('iprs,pst->irt', chosen, factor, precision=highest_accuracy)
        carried = jnp.einsum('irs,st->irt', parent_block, upper, precision=highest_accuracy)
        return -(carried + local_sum)

    column_two_full = lax.map(second_column, (pattern_two, lower_two, second_scaled_factor, parent_column))
    parent_slots = on_slots[parents]
    second_parent_inverse = -(jnp.einsum('mab,mbd->mad', diag_one[parents], second_scaled_factor, precision=highest_accuracy)
                  + jnp.einsum('mpsa,mpsb->mab', parent_slots, lower_two, precision=highest_accuracy))
    second_on_slots = jax.vmap(lambda z, s: z[s])(column_two_full, pattern_two)
    second_diagonal_inverse = (second_pivot_inverse - jnp.einsum('oik,oiu->oku', second_scaled_factor, second_parent_inverse, precision=highest_accuracy)
                - jnp.einsum('mpsa,mpsb->mab', lower_two, second_on_slots, precision=highest_accuracy))
    column_one = column_full.reshape(K1, NA * B, B)
    column_two = column_two_full.reshape(M2, NA * B, B)
    return (column_one, diag_one, column_two, second_parent_inverse, second_diagonal_inverse)
```

```python
import functools

import jax
import jax.numpy as jnp
from jax import lax
from jax.experimental import pallas as pl
from jax.experimental.pallas import tpu as pltpu
from jax.sharding import PartitionSpec as P

MESH = pl.DeviceIdType.MESH
CORES = 2


def split_dot(left, right, transposed):
    contract = (((0,), (0,)), ((), ())) if transposed else (((1,), (0,)), ((), ()))
    dot = functools.partial(
        lax.dot_general, dimension_numbers=contract, preferred_element_type=jnp.float32
    )
    left_hi, right_hi = left.astype(jnp.bfloat16), right.astype(jnp.bfloat16)
    left_lo = (left - left_hi.astype(jnp.float32)).astype(jnp.bfloat16)
    right_lo = (right - right_hi.astype(jnp.float32)).astype(jnp.bfloat16)
    return dot(left_hi, right_lo) + dot(left_lo, right_hi) + dot(left_hi, right_hi)


def product_kernel(transposed, masked, add, left_index, right_index, keep, left, right, *rest):
    out = rest[-1]
    value = split_dot(left[0], right[0], transposed)
    if masked:
        value = jnp.where(keep[pl.program_id(0)] > 0, value, 0.0)
    if add:
        value = rest[0][0] - value
    out[0] = value


def products(left, left_index, right, right_index, transposed=False, keep=None, minus_from=None):
    count = left_index.shape[0]
    width = left.shape[1]
    masked = keep is not None
    if keep is None:
        keep = left_index
    block = (1, width, width)
    specs = [
        pl.BlockSpec(block, lambda g, a, b, k: (a[g], 0, 0)),
        pl.BlockSpec(block, lambda g, a, b, k: (b[g], 0, 0)),
    ]
    args = [left, right]
    if minus_from is not None:
        specs.append(pl.BlockSpec(block, lambda g, a, b, k: (g, 0, 0)))
        args.append(minus_from)
    return pl.pallas_call(
        functools.partial(product_kernel, transposed, masked, minus_from is not None),
        out_shape=jax.ShapeDtypeStruct((count, width, width), jnp.float32),
        grid_spec=pltpu.PrefetchScalarGridSpec(
            num_scalar_prefetch=3,
            grid=(count,),
            in_specs=specs,
            out_specs=pl.BlockSpec(block, lambda g, a, b, k: (g, 0, 0)),
        ),
    )(left_index.astype(jnp.int32), right_index.astype(jnp.int32), keep.astype(jnp.int32), *args)


def exchange_kernel(kinds, rows, cols, *refs):
    count = len(kinds)
    sources, targets = refs[:count], refs[count : 2 * count]
    sems = refs[2 * count :]
    row, col = lax.axis_index("prow"), lax.axis_index("pcol")
    per = cols // rows
    chips = cols // CORES
    chip, core = col // CORES, lax.rem(col, CORES)
    partner = chip * CORES + (1 - core)
    own_place, home = lax.rem(col, per), col // per
    used = [axis for _, axis in kinds]

    barrier = pltpu.get_barrier_semaphore()
    expected = 0
    if "pcol" in used:
        for d in range(1, cols):
            pl.semaphore_signal(
                barrier, inc=1, device_id=(row, lax.rem(col + d, cols)), device_id_type=MESH
            )
        expected += cols - 1
    if "prow" in used:
        for d in range(1, rows):
            pl.semaphore_signal(
                barrier, inc=1, device_id=(lax.rem(row + d, rows), col), device_id_type=MESH
            )
        expected += rows - 1
    if "both" in used:
        for b in range(per):

            @pl.when(home != row)
            def _():
                pl.semaphore_signal(
                    barrier, inc=1, device_id=(home, row * per + b), device_id_type=MESH
                )

            if "pcol" not in used:

                @pl.when(jnp.logical_and(home == row, b != own_place))
                def _():
                    pl.semaphore_signal(
                        barrier, inc=1, device_id=(home, row * per + b), device_id_type=MESH
                    )

    if "both" in used:
        near = 0 if "pcol" in used else per - 1
        pl.semaphore_wait(barrier, expected + jnp.where(home != row, per, near))
    else:
        pl.semaphore_wait(barrier, expected)

    def remote(source, target, send, recv, device):
        return pltpu.make_async_remote_copy(
            src_ref=source,
            dst_ref=target,
            send_sem=send,
            recv_sem=recv,
            device_id=device,
            device_id_type=MESH,
        )

    copies, forwards, locals_ = [], [], []
    for op, (kind, axis) in enumerate(kinds):
        x, out = sources[op], targets[op]
        send, recv = sems[2 * op], sems[2 * op + 1]
        if kind == "transpose":
            continue
        size, me = (rows, row) if axis == "prow" else (cols, col)
        if kind == "gather" and axis == "pcol":
            for d in range(1, chips):
                there = lax.rem(chip + d, chips) * CORES + core
                copy = remote(x, out.at[me], send.at[d], recv.at[d], (row, there))
                copy.start()
                here = lax.rem(chip + chips - d, chips) * CORES + core
                forwards.append((copy, op, d, here))
            copy = remote(x, out.at[me], send.at[0], recv.at[0], (row, partner))
            copy.start()
            copies.append(copy)
        else:
            for d in range(1, size):
                there = lax.rem(me + d, size)
                device = (there, col) if axis == "prow" else (row, there)
                source = x if kind == "gather" else x.at[there]
                copy = remote(source, out.at[me], send.at[d], recv.at[d], device)
                copy.start()
                copies.append(copy)
        mine = x if kind == "gather" else x.at[me]
        local = pltpu.make_async_copy(mine, out.at[me], sems[2 * count].at[op])
        local.start()
        locals_.append(local)

    def away(op, b):
        return remote(
            sources[op],
            targets[op].at[own_place],
            sems[2 * op].at[b],
            sems[2 * op + 1].at[own_place],
            (home, row * per + b),
        )

    def near_copy(op, place):
        return pltpu.make_async_copy(
            sources[op], targets[op].at[place], sems[2 * op + 1].at[place]
        )

    def stays(b):
        return jnp.logical_and(home == row, b == own_place)

    transposes = [op for op, (kind, _) in enumerate(kinds) if kind == "transpose"]
    for op in transposes:
        for b in range(per):

            @pl.when(stays(b))
            def _():
                near_copy(op, own_place).start()

            @pl.when(jnp.logical_not(stays(b)))
            def _():
                away(op, b).start()

    for copy, op, d, here in forwards:
        copy.wait_recv()
        out = targets[op]
        forward = remote(
            out.at[here],
            out.at[here],
            sems[2 * op].at[chips - 1 + d],
            sems[2 * op + 1].at[chips - 1 + d],
            (row, partner),
        )
        forward.start()
        copies.append(forward)
    for copy, _, _, _ in forwards:
        copy.wait_send()
    for copy in copies:
        copy.wait_send()
        copy.wait_recv()
    for local in locals_:
        local.wait()
    for op in transposes:
        for b in range(per):

            @pl.when(jnp.logical_not(stays(b)))
            def _():
                away(op, b).wait_send()

        for a in range(per):
            near_copy(op, a).wait()


def exchange(number, *ops):
    rows, cols = lax.axis_size("prow"), lax.axis_size("pcol")
    shapes, scratch, kinds = [], [], []
    for kind, axis, x in ops:
        size = {"prow": rows, "pcol": cols, "both": cols // rows}[axis]
        lead = x.shape if kind != "all" else x.shape[1:]
        shapes.append(jax.ShapeDtypeStruct((size,) + lead, x.dtype))
        scratch += [pltpu.SemaphoreType.DMA((size,))] * 2
        kinds.append((kind, axis))
    scratch.append(pltpu.SemaphoreType.DMA((len(ops),)))
    anywhere = pl.BlockSpec(memory_space=pl.ANY)
    return pl.pallas_call(
        functools.partial(exchange_kernel, tuple(kinds), rows, cols),
        out_shape=shapes,
        in_specs=[anywhere] * len(ops),
        out_specs=[anywhere] * len(ops),
        scratch_shapes=scratch,
        compiler_params=pltpu.CompilerParams(collective_id=number, has_side_effects=True),
    )(*[x for _, _, x in ops])


def body(
    anc_inverse,
    pattern_one,
    parents,
    low_one,
    pivot_one,
    low_two,
    second_scaled_factor,
    second_pivot_inverse,
):
    row, col = lax.axis_index("prow"), lax.axis_index("pcol")
    rows, cols = lax.axis_size("prow"), lax.axis_size("pcol")
    per = cols // rows
    width = pivot_one.shape[1]
    piece = width // cols
    owned = anc_inverse.shape[1] // width
    zblocks = anc_inverse.reshape(width, owned, width).transpose(1, 0, 2)
    everyone = jnp.arange(cols, dtype=jnp.int32)
    mine = jnp.arange(per, dtype=jnp.int32)
    zero = jnp.zeros((1,), jnp.int32)
    place = col // per
    child = jnp.zeros((cols,), jnp.int32).at[parents].set(everyone)
    row_slots = lax.dynamic_index_in_dim(pattern_one, row, 1, keepdims=False) - row * owned
    row_slots_two = jnp.take(row_slots, parents)
    place_slots = lax.dynamic_index_in_dim(pattern_one, place, 1, keepdims=False)
    hit_one = lax.dynamic_slice_in_dim(place_slots, row * per, per) == col
    hit_two = lax.dynamic_slice_in_dim(jnp.take(place_slots, parents), row * per, per) == col
    one, two = low_one[0], low_two[0]

    def pieces(blocks):
        return blocks.reshape(per, cols, piece, width).transpose(1, 0, 2, 3)

    lowall, one_t, two_t, pivot_pieces = exchange(
        0,
        ("gather", "pcol", one),
        ("transpose", "both", one),
        ("transpose", "both", two),
        ("all", "pcol", pivot_one.reshape(cols, piece, width)),
    )
    parent_index = lax.dynamic_slice_in_dim(parents, col, 1)
    merged = products(lowall, parent_index, second_scaled_factor, zero, minus_from=low_two)[0]
    first_terms = products(zblocks, row_slots, lowall, everyone)
    mergedall, first_got = exchange(
        1,
        ("gather", "pcol", merged),
        ("all", "prow", first_terms.reshape(rows, per, width, width)),
    )
    column_one = -jnp.sum(first_got, axis=0)
    pivot_terms = products(one_t, mine, column_one, mine, transposed=True, keep=hit_one)
    second_terms = products(zblocks, row_slots_two, mergedall, everyone)
    of_child = lax.dynamic_index_in_dim(
        mergedall, lax.dynamic_index_in_dim(child, col, 0, keepdims=False), 0, keepdims=False
    )
    second_got, child_t, pivot_got = exchange(
        2,
        ("all", "prow", second_terms.reshape(rows, per, width, width)),
        ("transpose", "both", of_child),
        ("all", "pcol", pieces(pivot_terms)),
    )
    column_two = -jnp.sum(second_got, axis=0)
    pivot_piece = jnp.sum(pivot_got, axis=0)
    cross_terms = products(column_one, mine, child_t, mine, transposed=True, keep=hit_one)
    diag_terms = products(two_t, mine, column_two, mine, transposed=True, keep=hit_two)
    small_got, pivot_rows = exchange(
        3,
        ("all", "pcol", jnp.concatenate([pieces(cross_terms), pieces(diag_terms)], axis=1)),
        ("gather", "prow", pivot_piece),
    )
    pivot_rows = pivot_rows.reshape(cols, piece, width)
    small_rows, pivot_final = exchange(
        4,
        ("gather", "prow", jnp.sum(small_got, axis=0)),
        (
            "all",
            "pcol",
            jnp.stack(
                [
                    pivot_rows,
                    jnp.take(pivot_rows, parents, axis=0),
                    jnp.take(pivot_pieces, parents, axis=0),
                ],
                axis=1,
            ),
        ),
    )
    cross_rows = small_rows[:, :per].reshape(cols, piece, width)
    diag_rows = small_rows[:, per:].reshape(cols, piece, width)
    (small_final,) = exchange(
        5,
        ("all", "pcol", jnp.stack([jnp.take(cross_rows, parents, axis=0), diag_rows], axis=1)),
    )

    def whole(array, index):
        return array[:, index].reshape(1, width, width)

    diag_one = pivot_one - whole(pivot_final, 0)
    parent_sum = whole(pivot_final, 1)
    left = whole(pivot_final, 2) - parent_sum + parent_sum.transpose(0, 2, 1)
    second_parent_inverse = products(
        left, zero, second_scaled_factor, zero, minus_from=-whole(small_final, 0)
    )
    second_diagonal_inverse = products(
        second_scaled_factor,
        zero,
        second_parent_inverse,
        zero,
        transposed=True,
        minus_from=second_pivot_inverse - whole(small_final, 1),
    )
    return (column_one, diag_one, column_two, second_parent_inverse, second_diagonal_inverse)


def solution(mesh):
    placed = (
        P("pcol", "prow"),
        P(),
        P(),
        P("pcol", "prow", None),
        P("pcol", None, None),
        P("pcol", "prow", None),
        P("pcol", None, None),
        P("pcol", None, None),
    )
    return jax.shard_map(
        body,
        mesh=mesh,
        in_specs=placed,
        out_specs=(
            P("prow", "pcol", None),
            P("pcol", None, None),
            P("prow", "pcol", None),
            P("pcol", None, None),
            P("pcol", None, None),
        ),
        check_vma=False,
    )
```

```python
import functools

import jax
import jax.numpy as jnp
from jax import lax
from jax.experimental import pallas as pl
from jax.experimental.pallas import tpu as pltpu
from jax.sharding import PartitionSpec as P

MESH = pl.DeviceIdType.MESH
CORES = 2


def split_dot(left, right, transposed):
    contract = (((0,), (0,)), ((), ())) if transposed else (((1,), (0,)), ((), ()))
    dot = functools.partial(
        lax.dot_general, dimension_numbers=contract, preferred_element_type=jnp.float32
    )
    left_hi, right_hi = left.astype(jnp.bfloat16), right.astype(jnp.bfloat16)
    left_lo = (left - left_hi.astype(jnp.float32)).astype(jnp.bfloat16)
    right_lo = (right - right_hi.astype(jnp.float32)).astype(jnp.bfloat16)
    return dot(left_hi, right_lo) + dot(left_lo, right_hi) + dot(left_hi, right_hi)


def product_kernel(transposed, keep_at, negate, prefetched, *refs):
    left, right, out = refs[prefetched], refs[prefetched + 1], refs[-1]
    value = split_dot(left[0], right[0], transposed)
    if keep_at is not None:
        value = jnp.where(refs[keep_at][pl.program_id(0)] > 0, value, 0.0)
    if len(refs) > prefetched + 3:
        value = refs[prefetched + 2][0] - value
    elif negate:
        value = -value
    out[0] = value


def products(
    count, left, right, left_index=None, right_index=None, transposed=False, keep=None,
    minus_from=None, negate=False,
):
    width = left.shape[1]
    block = (1, width, width)
    prefetch = []

    def chosen(index):
        if index is None:
            return pl.BlockSpec(block, lambda g, *p: (g, 0, 0))
        at = len(prefetch)
        prefetch.append(index.astype(jnp.int32))
        return pl.BlockSpec(block, lambda g, *p: (p[at][g], 0, 0))

    specs = [chosen(left_index), chosen(right_index)]
    args = [left, right]
    if minus_from is not None:
        specs.append(chosen(None))
        args.append(minus_from)
    keep_at = None
    if keep is not None:
        keep_at = len(prefetch)
        prefetch.append(keep.astype(jnp.int32))
    return pl.pallas_call(
        functools.partial(product_kernel, transposed, keep_at, negate, len(prefetch)),
        out_shape=jax.ShapeDtypeStruct((count, width, width), jnp.float32),
        grid_spec=pltpu.PrefetchScalarGridSpec(
            num_scalar_prefetch=len(prefetch),
            grid=(count,),
            in_specs=specs,
            out_specs=chosen(None),
        ),
    )(*prefetch, *args)


def exchange_kernel(kinds, rows, cols, *refs):
    count = len(kinds)
    sources, targets = refs[:count], refs[count : 2 * count]
    sems = refs[2 * count :]
    row, col = lax.axis_index("prow"), lax.axis_index("pcol")
    per = cols // rows
    chips = cols // CORES
    chip, core = col // CORES, lax.rem(col, CORES)
    partner = chip * CORES + (1 - core)
    own_place, home = lax.rem(col, per), col // per
    used = [axis for _, axis in kinds]

    barrier = pltpu.get_barrier_semaphore()
    expected = 0
    if "pcol" in used:
        for d in range(1, cols):
            pl.semaphore_signal(
                barrier, inc=1, device_id=(row, lax.rem(col + d, cols)), device_id_type=MESH
            )
        expected += cols - 1
    if "prow" in used:
        for d in range(1, rows):
            pl.semaphore_signal(
                barrier, inc=1, device_id=(lax.rem(row + d, rows), col), device_id_type=MESH
            )
        expected += rows - 1
    if "both" in used:

        @pl.when(home != row)
        def _():
            pl.semaphore_signal(
                barrier, inc=1, device_id=(home, row * per + own_place), device_id_type=MESH
            )

        expected += jnp.where(home != row, 1, 0)
    pl.semaphore_wait(barrier, expected)

    def remote(source, target, send, recv, device):
        return pltpu.make_async_remote_copy(
            src_ref=source,
            dst_ref=target,
            send_sem=send,
            recv_sem=recv,
            device_id=device,
            device_id_type=MESH,
        )

    copies, forwards, locals_ = [], [], []
    for op, (kind, axis) in enumerate(kinds):
        x, out = sources[op], targets[op]
        send, recv = sems[2 * op], sems[2 * op + 1]
        if kind == "transpose":
            continue
        size, me = (rows, row) if axis == "prow" else (cols, col)
        if kind == "gather" and axis == "pcol":
            for d in range(1, chips):
                there = lax.rem(chip + d, chips) * CORES + core
                copy = remote(x, out.at[me], send.at[d], recv.at[d], (row, there))
                copy.start()
                here = lax.rem(chip + chips - d, chips) * CORES + core
                forwards.append((copy, op, d, here))
            copy = remote(x, out.at[me], send.at[0], recv.at[0], (row, partner))
            copy.start()
            copies.append(copy)
        else:
            for d in range(1, size):
                there = lax.rem(me + d, size)
                device = (there, col) if axis == "prow" else (row, there)
                source = x if kind == "gather" else x.at[there]
                copy = remote(source, out.at[me], send.at[d], recv.at[d], device)
                copy.start()
                copies.append(copy)
        mine = x if kind == "gather" else x.at[me]
        local = pltpu.make_async_copy(mine, out.at[me], sems[2 * count].at[op])
        local.start()
        locals_.append(local)

    def away(op):
        return remote(
            sources[op],
            targets[op].at[own_place],
            sems[2 * op].at[0],
            sems[2 * op + 1].at[0],
            (home, row * per + own_place),
        )

    def near(op):
        return pltpu.make_async_copy(
            sources[op], targets[op].at[own_place], sems[2 * op + 1].at[0]
        )

    transposes = [op for op, (kind, _) in enumerate(kinds) if kind == "transpose"]
    for op in transposes:

        @pl.when(home == row)
        def _():
            near(op).start()

        @pl.when(home != row)
        def _():
            away(op).start()

    for copy, op, d, here in forwards:
        copy.wait_recv()
        out = targets[op]
        forward = remote(
            out.at[here],
            out.at[here],
            sems[2 * op].at[chips - 1 + d],
            sems[2 * op + 1].at[chips - 1 + d],
            (row, partner),
        )
        forward.start()
        copies.append(forward)
    for op in transposes:
        near(op).wait()

        @pl.when(home != row)
        def _():
            away(op).wait_send()

        out = targets[op]
        for d in range(1, per):
            there = home * per + lax.rem(own_place + d, per)
            forward = remote(
                out.at[own_place],
                out.at[own_place],
                sems[2 * op].at[d],
                sems[2 * op + 1].at[d],
                (row, there),
            )
            forward.start()
            copies.append(forward)
    for copy, _, _, _ in forwards:
        copy.wait_send()
    for copy in copies:
        copy.wait_send()
        copy.wait_recv()
    for local in locals_:
        local.wait()
def exchange(number, *ops):
    rows, cols = lax.axis_size("prow"), lax.axis_size("pcol")
    shapes, scratch, kinds = [], [], []
    for kind, axis, x in ops:
        size = {"prow": rows, "pcol": cols, "both": cols // rows}[axis]
        lead = x.shape if kind != "all" else x.shape[1:]
        shapes.append(jax.ShapeDtypeStruct((size,) + lead, x.dtype))
        scratch += [pltpu.SemaphoreType.DMA((size,))] * 2
        kinds.append((kind, axis))
    scratch.append(pltpu.SemaphoreType.DMA((len(ops),)))
    anywhere = pl.BlockSpec(memory_space=pl.ANY)
    return pl.pallas_call(
        functools.partial(exchange_kernel, tuple(kinds), rows, cols),
        out_shape=shapes,
        in_specs=[anywhere] * len(ops),
        out_specs=[anywhere] * len(ops),
        scratch_shapes=scratch,
        compiler_params=pltpu.CompilerParams(collective_id=number, has_side_effects=True),
    )(*[x for _, _, x in ops])


def body(
    anc_inverse,
    pattern_one,
    parents,
    low_one,
    pivot_one,
    low_two,
    second_scaled_factor,
    second_pivot_inverse,
):
    row, col = lax.axis_index("prow"), lax.axis_index("pcol")
    rows, cols = lax.axis_size("prow"), lax.axis_size("pcol")
    per = cols // rows
    width = pivot_one.shape[1]
    piece = width // cols
    owned = anc_inverse.shape[1] // width
    zblocks = anc_inverse.reshape(width, owned, width).transpose(1, 0, 2)
    everyone = jnp.arange(cols, dtype=jnp.int32)
    place = col // per
    child = jnp.zeros((cols,), jnp.int32).at[parents].set(everyone)
    row_slots = lax.dynamic_index_in_dim(pattern_one, row, 1, keepdims=False) - row * owned
    row_slots_two = jnp.take(row_slots, parents)
    place_slots = lax.dynamic_index_in_dim(pattern_one, place, 1, keepdims=False)
    hit_one = lax.dynamic_slice_in_dim(place_slots, row * per, per) == col
    hit_two = lax.dynamic_slice_in_dim(jnp.take(place_slots, parents), row * per, per) == col
    one, two = low_one[0], low_two[0]

    def pieces(blocks):
        return blocks.reshape(per, cols, piece, width).transpose(1, 0, 2, 3)

    lowall, one_t, pivot_pieces = exchange(
        0,
        ("gather", "pcol", one),
        ("transpose", "both", one),
        ("all", "pcol", pivot_one.reshape(cols, piece, width)),
    )
    parent_index = lax.dynamic_slice_in_dim(parents, col, 1)
    merged = products(
        1, lowall, second_scaled_factor, left_index=parent_index, minus_from=low_two
    )[0]
    first_terms = products(cols, zblocks, lowall, left_index=row_slots, negate=True)
    mergedall, first_got, two_t, pivot_parent = exchange(
        1,
        ("gather", "pcol", merged),
        ("all", "prow", first_terms.reshape(rows, per, width, width)),
        ("transpose", "both", two),
        ("all", "pcol", jnp.take(pivot_pieces, parents, axis=0)),
    )
    column_one = jnp.sum(first_got, axis=0)
    pivot_terms = products(per, one_t, column_one, transposed=True, keep=hit_one)
    second_terms = products(
        cols, zblocks, mergedall, left_index=row_slots_two, negate=True
    )
    of_child = lax.dynamic_index_in_dim(
        mergedall, lax.dynamic_index_in_dim(child, col, 0, keepdims=False), 0, keepdims=False
    )
    second_got, child_t, pivot_got = exchange(
        2,
        ("all", "prow", second_terms.reshape(rows, per, width, width)),
        ("transpose", "both", of_child),
        ("all", "pcol", pieces(pivot_terms)),
    )
    column_two = jnp.sum(second_got, axis=0)
    pivot_piece = jnp.sum(pivot_got, axis=0)
    cross_terms = products(per, column_one, child_t, transposed=True, keep=hit_one)
    diag_terms = products(per, two_t, column_two, transposed=True, keep=hit_two)
    small_got, pivot_rows = exchange(
        3,
        ("all", "pcol", jnp.concatenate([pieces(cross_terms), pieces(diag_terms)], axis=1)),
        ("gather", "prow", pivot_piece),
    )
    pivot_rows = pivot_rows.reshape(cols, piece, width)
    small_rows, pivot_final = exchange(
        4,
        ("gather", "prow", jnp.sum(small_got, axis=0)),
        (
            "all",
            "pcol",
            jnp.stack([pivot_rows, jnp.take(pivot_rows, parents, axis=0)], axis=1),
        ),
    )
    cross_rows = small_rows[:, :per].reshape(cols, piece, width)
    diag_rows = small_rows[:, per:].reshape(cols, piece, width)
    (small_final,) = exchange(
        5,
        ("all", "pcol", jnp.stack([jnp.take(cross_rows, parents, axis=0), diag_rows], axis=1)),
    )

    def whole(array, index):
        return array[:, index].reshape(1, width, width)

    diag_one = pivot_one - whole(pivot_final, 0)
    parent_sum = whole(pivot_final, 1)
    left = pivot_parent.reshape(1, width, width) - parent_sum + parent_sum.transpose(0, 2, 1)
    second_parent_inverse = products(
        1, left, second_scaled_factor, minus_from=-whole(small_final, 0)
    )
    second_diagonal_inverse = products(
        1,
        second_scaled_factor,
        second_parent_inverse,
        transposed=True,
        minus_from=second_pivot_inverse - whole(small_final, 1),
    )
    return (column_one, diag_one, column_two, second_parent_inverse, second_diagonal_inverse)


def solution(mesh):
    placed = (
        P("pcol", "prow"),
        P(),
        P(),
        P("pcol", "prow", None),
        P("pcol", None, None),
        P("pcol", "prow", None),
        P("pcol", None, None),
        P("pcol", None, None),
    )
    return jax.shard_map(
        body,
        mesh=mesh,
        in_specs=placed,
        out_specs=(
            P("prow", "pcol", None),
            P("pcol", None, None),
            P("prow", "pcol", None),
            P("pcol", None, None),
            P("pcol", None, None),
        ),
        check_vma=False,
    )
```
